32 devices in a mesh: kx: 4 (over y, x), ky: 4 (over z), kz: 2 (over core).
Axes of the slice: x: 2, y: 2, z: 4, core: 2. Of those that a mesh axis runs over, the one named last changes fastest.
Arguments:
- orbitals: bfloat16 [16, 16, 2, 1024, 128], P('kx', 'ky', 'kz'), may hold values from -6 to 6
- kernel: bfloat16 [32, 2, 1024, 1024], P(('kx', 'ky', 'kz')), may hold values from -0.00015258789 to 0.00015258789
- plan: int32 [2, 2, 32], replicated, may hold values from 0 to 15, as said below
- occupation: int32 [16, 16, 2, 64], replicated, may hold values 0 or 1
Outputs:
- exchange_blocks: float32 [16, 16, 2, 64, 128], P('kx', 'ky', 'kz')
The draws below stay inside these ranges and needn't reach their ends.
Inputs may be any that keep to these rules, and one draw needn't show every extreme that they name: `plan`: entry [r, 0, e] is the slot, in device e's block of 4 x 4 x 1 k-points, of the k-point that e sends as k in round r, and [r, 1, e] the slot of the one it sends as p. For every owner, k minus p is the same momentum transfer on the periodic k-mesh in every round.
All inputs are finite; a program needn't handle non-finite values.
Results may differ from the reference program's by a relative error of at most 0.004.
Values may be sent and summed in bfloat16 or wider, within the bound.
No kernel may reach another device: no remote copies, remote signals or barrier semaphores. Data moves between devices by JAX's collectives and lax.ppermute only.
A program may use at most 128 MiB of HBM per device.

```python
import jax
import jax.numpy as jnp
from jax import lax

NMU = 1024
NB = 64
CX = 4
CY = 4
CZ = 1
ROUNDS = 2
MX = 16
MY = 16
MZ = 2
OWNERS = 32
N_KX = 4
N_KY = 4
N_KZ = 2


def hop_shifts_drawn(turn_number, mesh_counts):
    forward = ((turn_number + 1) % mesh_counts[0], (2 * turn_number + 1) % mesh_counts[1], (3 * turn_number + 1) % mesh_counts[2])
    partner = (forward[0], forward[1], (forward[2] - mesh_counts[2] // 2) % mesh_counts[2])
    return (forward, partner)


def sender_linear(owner_coords, shift, mesh_counts):
    sender_first = (owner_coords[0] - shift[0]) % mesh_counts[0]
    sender_second = (owner_coords[1] - shift[1]) % mesh_counts[1]
    sender_third = (owner_coords[2] - shift[2]) % mesh_counts[2]
    return (sender_first * mesh_counts[1] + sender_second) * mesh_counts[2] + sender_third


def draw_plan(key, part):
    mesh_counts = (N_KX, N_KY, N_KZ)
    cell_counts = (CX, CY, CZ)
    owner_total = N_KX * N_KY * N_KZ
    owners = jnp.arange(owner_total, dtype=jnp.int32)
    owner_coords = (owners // (N_KY * N_KZ), owners // N_KZ % N_KY, owners % N_KZ)
    offsets = []
    for dimension in range(3):
        offsets.append(jax.random.randint(jax.random.fold_in(key, 100 + dimension), (owner_total,), -(cell_counts[dimension] - 1), cell_counts[dimension]))
    rows_out = []
    for turn_number in range(ROUNDS):
        forward, partner = hop_shifts_drawn(turn_number, mesh_counts)
        first_cells = []
        second_cells = []
        for dimension in range(3):
            lowest = jnp.maximum(0, -offsets[dimension])
            highest = cell_counts[dimension] - jnp.maximum(0, offsets[dimension])
            chosen = jax.random.randint(jax.random.fold_in(key, 1000 * turn_number + dimension + 7), (owner_total,), lowest, highest)
            second_cells.append(chosen)
            first_cells.append(chosen + offsets[dimension])
        first_slot = (first_cells[0] * CY + first_cells[1]) * CZ + first_cells[2]
        second_slot = (second_cells[0] * CY + second_cells[1]) * CZ + second_cells[2]
        first_row = jnp.zeros((owner_total,), jnp.int32).at[sender_linear(owner_coords, forward, mesh_counts)].set(first_slot.astype(jnp.int32))
        second_row = jnp.zeros((owner_total,), jnp.int32).at[sender_linear(owner_coords, partner, mesh_counts)].set(second_slot.astype(jnp.int32))
        rows_out.append(jnp.stack([first_row, second_row]))
    return jnp.stack(rows_out).astype(jnp.int32)


def with_ends(entries, rng, smallest, top_value):
    longest = entries.shape.index(max(entries.shape))
    spots = []
    for shift in (0, 1):
        where = [jax.random.randint(jax.random.fold_in(rng, axis), (), 0, length) for axis, length in enumerate(entries.shape)]
        where[longest] = (where[longest] + shift) % entries.shape[longest]
        spots.append(tuple(where))
    return entries.at[spots[0]].set(smallest).at[spots[1]].set(top_value)


def levels(key, dims, shards, least, largest):
    loudness = 1.0
    for position, parts in shards:
        heights = jax.random.uniform(jax.random.fold_in(jax.random.fold_in(key, 6), position), (parts,), jnp.float32, least / len(shards), largest / len(shards))
        loudness = loudness * jnp.repeat(jnp.exp(heights), dims[position] // parts).reshape((-1,) + (1,) * (len(dims) - 1 - position))
    return loudness


def bell_draw(stream_key, extent, spread, reach, shards=(), held_as=jnp.bfloat16):
    loudness = levels(stream_key, extent, shards, -0.22, 0.18) if shards else 1.0
    array = jax.random.normal(stream_key, extent, jnp.float32) * spread * loudness
    return jnp.minimum(jnp.maximum(array, -reach), reach).astype(held_as)


def setup_inputs(seed: int = 0) -> dict:
    streams_of = jax.random.split(jax.random.key(seed), 5)
    orbitals = bell_draw(streams_of[0], (MX, MY, MZ, NMU, 2 * NB), 1.0, 6.0, ((0, 4), (1, 4), (2, 2)))
    kernel = bell_draw(streams_of[1], (OWNERS, 2, NMU, NMU), (25 * NMU * NMU * NB) ** -0.5, 0.00015258789, ((0, 32),))
    plan = draw_plan(jax.random.fold_in(streams_of[4], 71), 0)
    occupation = with_ends((jax.random.randint(streams_of[3], (MX, MY, MZ, NB), 0, 4) < 3).astype(jnp.int32), jax.random.fold_in(streams_of[3], 1), 0, 1)
    return dict(orbitals=orbitals, kernel=kernel, plan=plan, occupation=occupation)


def hop_shifts(turn_number, mesh_counts):
    forward = ((turn_number + 1) % mesh_counts[0], (2 * turn_number + 1) % mesh_counts[1], (3 * turn_number + 1) % mesh_counts[2])
    partner = (forward[0], forward[1], (forward[2] - mesh_counts[2] // 2) % mesh_counts[2])
    return forward, partner


def global_points(plan, turn_number, column, shift, owner_coords, mesh_counts, cell_counts):
    sender_first = (owner_coords[0] - shift[0]) % mesh_counts[0]
    sender_second = (owner_coords[1] - shift[1]) % mesh_counts[1]
    sender_third = (owner_coords[2] - shift[2]) % mesh_counts[2]
    linear = (sender_first * mesh_counts[1] + sender_second) * mesh_counts[2] + sender_third
    slot_index = plan[turn_number, column, linear]
    cell_first = slot_index // (cell_counts[1] * cell_counts[2])
    cell_second = (slot_index // cell_counts[2]) % cell_counts[1]
    cell_third = slot_index % cell_counts[2]
    return (sender_first * cell_counts[0] + cell_first, sender_second * cell_counts[1] + cell_second, sender_third * cell_counts[2] + cell_third)


def density_product(orbital, occupied):
    bands = orbital.shape[1] // 2
    weights = jnp.concatenate([occupied, occupied]).astype(orbital.dtype)
    masked = orbital * weights[None, :]
    swapped = jnp.concatenate([-orbital[:, bands:], orbital[:, :bands]], axis=1)
    density_real = jnp.dot(masked, orbital.T, preferred_element_type=jnp.float32)
    density_imag = jnp.dot(masked, swapped.T, preferred_element_type=jnp.float32)
    return density_real, density_imag


def kernel_hadamard(kernel_real, kernel_imag, density_real, density_imag, conjugate_sign):
    weight_real = kernel_real.astype(jnp.float32)
    weight_imag = kernel_imag.astype(jnp.float32) * conjugate_sign
    hadamard_real = weight_real * density_real - weight_imag * density_imag
    hadamard_imag = weight_real * density_imag + weight_imag * density_real
    return jnp.concatenate([hadamard_real, hadamard_imag], axis=1).astype(jnp.bfloat16)


def exchange_block(stacked, orbital):
    bands = orbital.shape[1] // 2
    real_part = orbital[:, :bands]
    imag_part = orbital[:, bands:]
    blocked = jnp.concatenate([orbital, jnp.concatenate([-imag_part, real_part], axis=1)], axis=0)
    mixture = jnp.dot(stacked, blocked, preferred_element_type=jnp.float32).astype(jnp.bfloat16)
    gram_matrix = lax.dot_general(orbital, mixture, (((0,), (0,)), ((), ())), preferred_element_type=jnp.float32)
    result_real = -(gram_matrix[:bands, :bands] + gram_matrix[bands:, bands:])
    result_imag = -(gram_matrix[:bands, bands:] - gram_matrix[bands:, :bands])
    return jnp.concatenate([result_real, result_imag], axis=1)


def pair_blocks(kernel_real, kernel_imag, orbital_first, occupied_first, orbital_second, occupied_second):
    second_real, second_imag = density_product(orbital_second, occupied_second)
    first_block = exchange_block(kernel_hadamard(kernel_real, kernel_imag, second_real, second_imag, 1.0), orbital_first)
    first_real, first_imag = density_product(orbital_first, occupied_first)
    second_block = exchange_block(kernel_hadamard(kernel_real, kernel_imag, first_real, first_imag, -1.0), orbital_second)
    return first_block, second_block


def reference(orbitals, kernel, plan, occupation):
    mesh_counts = (N_KX, N_KY, N_KZ)
    cell_counts = (CX, CY, CZ)
    owner_total = N_KX * N_KY * N_KZ
    extent_second = CY * N_KY
    extent_third = CZ * N_KZ
    point_total = CX * N_KX * extent_second * extent_third
    flat_orbitals = orbitals.reshape(point_total, NMU, 2 * NB)
    flat_occupied = occupation.reshape(point_total, NB)
    owners = jnp.arange(owner_total, dtype=jnp.int32)
    owner_coords = (owners // (N_KY * N_KZ), (owners // N_KZ) % N_KY, owners % N_KZ)
    totals = jnp.zeros((point_total, NB, 2 * NB), jnp.float32)
    for turn_number in range(ROUNDS):
        forward, partner = hop_shifts(turn_number, mesh_counts)
        first_point = global_points(plan, turn_number, 0, forward, owner_coords, mesh_counts, cell_counts)
        second_point = global_points(plan, turn_number, 1, partner, owner_coords, mesh_counts, cell_counts)
        first_linear = ((first_point[0] * extent_second + first_point[1]) * extent_third + first_point[2]).astype(jnp.int32)
        second_linear = ((second_point[0] * extent_second + second_point[1]) * extent_third + second_point[2]).astype(jnp.int32)

        def one_owner(inputs):
            owner, first_index, second_index = inputs
            local_kernel = kernel[owner]
            return pair_blocks(local_kernel[0], local_kernel[1], flat_orbitals[first_index], flat_occupied[first_index], flat_orbitals[second_index], flat_occupied[second_index])

        first_blocks, second_blocks = lax.map(one_owner, (owners, first_linear, second_linear))
        totals = totals.at[first_linear].add(first_blocks)
        totals = totals.at[second_linear].add(second_blocks)
    return totals.reshape(CX * N_KX, extent_second, extent_third, NB, 2 * NB)
```

```python
import functools

import jax
import jax.numpy as jnp
from jax import lax
from jax.experimental import pallas as pl
from jax.experimental.pallas import tpu as pltpu
from jax.sharding import PartitionSpec as P

AXES = ("kx", "ky", "kz")
SMALL_GRANT = 4 << 20
PICK_GRANT = 61 << 20
PAIR_GRANT = 24 << 20
CONTRACT_LAST = (((1,), (1,)), ((), ()))
CONTRACT_FIRST = (((0,), (0,)), ((), ()))


def mesh_sizes():
    return tuple(lax.axis_size(axis) for axis in AXES)


def hop_shifts(turn_number, mesh_counts):
    forward = (
        (turn_number + 1) % mesh_counts[0],
        (2 * turn_number + 1) % mesh_counts[1],
        (3 * turn_number + 1) % mesh_counts[2],
    )
    partner = (forward[0], forward[1], (forward[2] - mesh_counts[2] // 2) % mesh_counts[2])
    return (forward, partner)


def linear_of(places, mesh_counts):
    return (places[0] * mesh_counts[1] + places[1]) * mesh_counts[2] + places[2]


def moved(block, shift, mesh_counts):
    route = []
    for first in range(mesh_counts[0]):
        for second in range(mesh_counts[1]):
            for third in range(mesh_counts[2]):
                target = tuple(
                    (place + step) % count
                    for place, step, count in zip((first, second, third), shift, mesh_counts)
                )
                route.append(
                    (linear_of((first, second, third), mesh_counts), linear_of(target, mesh_counts))
                )
    return lax.ppermute(block, AXES, route)


def negated(shift):
    return tuple(-step for step in shift)


def cell_of(slot, cell_counts):
    return (
        slot // (cell_counts[1] * cell_counts[2]),
        slot // cell_counts[2] % cell_counts[1],
        slot % cell_counts[2],
    )


def own_places():
    return tuple(lax.axis_index(axis) for axis in AXES)


def wrapped(value, count):
    return jnp.where(value < 0, value + count, value)


def whole(space):
    return pl.BlockSpec(memory_space=space)


def pick_kernel(turn_number, mesh_counts, plan_ref, orbitals_ref, first_ref, second_ref, sems):
    own = linear_of(own_places(), mesh_counts)
    copies = []
    for column, out_ref in ((1, second_ref), (0, first_ref)):
        cell = cell_of(plan_ref[turn_number, column, own], orbitals_ref.shape[:3])
        copy = pltpu.make_async_copy(
            orbitals_ref.at[cell[0], cell[1], cell[2]], out_ref, sems.at[column]
        )
        copy.start()
        copies.append(copy)
    for copy in copies:
        copy.wait()


def picked(turn_number, mesh_counts, plan, orbitals):
    block = jax.ShapeDtypeStruct(orbitals.shape[3:], orbitals.dtype)
    return pl.pallas_call(
        functools.partial(pick_kernel, turn_number, mesh_counts),
        out_shape=(block, block),
        in_specs=[whole(pltpu.SMEM), whole(pl.ANY)],
        out_specs=(whole(pltpu.VMEM), whole(pltpu.VMEM)),
        scratch_shapes=[pltpu.SemaphoreType.DMA((2,))],
        compiler_params=pltpu.CompilerParams(vmem_limit_bytes=PICK_GRANT),
        name=f"pick_{turn_number}",
    )(plan, orbitals)


def mask_kernel(mesh_counts, cell_counts, plan_ref, occupation_ref, out_ref, rows, sem):
    places = own_places()
    copies = []
    turns = plan_ref.shape[0]
    for turn_number in range(turns):
        for column, shift in enumerate(hop_shifts(turn_number, mesh_counts)):
            sender = tuple(
                wrapped(place - step, count)
                for place, step, count in zip(places, shift, mesh_counts)
            )
            cell = cell_of(plan_ref[turn_number, column, linear_of(sender, mesh_counts)], cell_counts)
            point = tuple(
                place * count + inner for place, count, inner in zip(sender, cell_counts, cell)
            )
            entry = 2 * turn_number + column
            copy = pltpu.make_async_copy(
                occupation_ref.at[point[0], point[1], pl.ds(point[2], 1)],
                rows.at[pl.ds(entry, 1)],
                sem.at[entry],
            )
            copy.start()
            copies.append(copy)
    for copy in copies:
        copy.wait()
    held = rows[...].astype(jnp.float32)
    out_ref[...] = jnp.concatenate([held, held], axis=1)


def masks_of(mesh_counts, cell_counts, plan, occupation):
    entries = plan.shape[0] * 2
    bands = occupation.shape[3]
    return pl.pallas_call(
        functools.partial(mask_kernel, mesh_counts, cell_counts),
        out_shape=jax.ShapeDtypeStruct((entries, 2 * bands), jnp.float32),
        in_specs=[whole(pltpu.SMEM), whole(pl.ANY)],
        out_specs=whole(pltpu.VMEM),
        scratch_shapes=[
            pltpu.VMEM((entries, bands), occupation.dtype),
            pltpu.SemaphoreType.DMA((entries,)),
        ],
        compiler_params=pltpu.CompilerParams(vmem_limit_bytes=SMALL_GRANT),
        name="masks",
    )(plan, occupation)


def quarter_turn(block):
    bands = block.shape[1] // 2
    return jnp.concatenate([-block[:, bands:], block[:, :bands]], axis=1)


def folded(gram):
    bands = gram.shape[0] // 2
    top, bottom = gram[:bands], gram[bands:]
    return -(top + jnp.concatenate([bottom[:, bands:], -bottom[:, :bands]], axis=1))


def dot32(left, right, dims):
    return lax.dot_general(left, right, dims, preferred_element_type=jnp.float32)


def pair_kernel(
    turn_number,
    chunk,
    mask_ref,
    kernel_ref,
    first_ref,
    second_ref,
    first_out,
    second_out,
    first_wide,
    second_wide,
    first_mix,
    second_mix,
):
    tile = kernel_ref.shape[2]
    points, width = first_ref.shape
    step = pl.program_id(0)

    @pl.when(step == 0)
    def _():
        for source, wide in ((first_ref, first_wide), (second_ref, second_wide)):
            block = source[...]
            wide[:points] = block
            wide[points:] = quarter_turn(block)

    rows = pl.ds(pl.multiple_of(step * tile, tile), tile)
    entry = 2 * turn_number
    first_masked = first_ref[rows, :] * mask_ref[entry : entry + 1, :].astype(first_ref.dtype)
    second_masked = second_ref[rows, :] * mask_ref[entry + 1 : entry + 2, :].astype(second_ref.dtype)
    first_total = jnp.zeros((tile, width), jnp.float32)
    second_total = first_total
    plain = (((1,), (0,)), ((), ()))
    for start in range(0, points, chunk):
        real = slice(start, start + chunk)
        imag = slice(points + start, points + start + chunk)
        weight_real = kernel_ref[0, 0, :, real].astype(jnp.float32)
        weight_imag = kernel_ref[0, 1, :, real].astype(jnp.float32)
        density_real = dot32(second_masked, second_wide[real], CONTRACT_LAST)
        density_imag = dot32(second_masked, second_wide[imag], CONTRACT_LAST)
        part_real = weight_real * density_real - weight_imag * density_imag
        part_imag = weight_real * density_imag + weight_imag * density_real
        first_total += dot32(part_real.astype(jnp.bfloat16), first_wide[real], plain)
        first_total += dot32(part_imag.astype(jnp.bfloat16), first_wide[imag], plain)
        density_real = dot32(first_masked, first_wide[real], CONTRACT_LAST)
        density_imag = dot32(first_masked, first_wide[imag], CONTRACT_LAST)
        part_real = weight_real * density_real + weight_imag * density_imag
        part_imag = weight_real * density_imag - weight_imag * density_real
        second_total += dot32(part_real.astype(jnp.bfloat16), second_wide[real], plain)
        second_total += dot32(part_imag.astype(jnp.bfloat16), second_wide[imag], plain)
    first_mix[rows, :] = first_total.astype(jnp.bfloat16)
    second_mix[rows, :] = second_total.astype(jnp.bfloat16)

    @pl.when(step == pl.num_programs(0) - 1)
    def _():
        for source, mix, out in (
            (first_ref, first_mix, first_out),
            (second_ref, second_mix, second_out),
        ):
            out[...] = folded(dot32(source[...], mix[...], CONTRACT_FIRST)).astype(out.dtype)


def pair_blocks(turn_number, masks, kernel, first, second):
    points, width = first.shape
    tile = points // 2
    fixed = lambda shape: pl.BlockSpec(shape, lambda step: (0,) * len(shape))
    block = jax.ShapeDtypeStruct((width // 2, width), jnp.bfloat16)
    return pl.pallas_call(
        functools.partial(pair_kernel, turn_number, points // 4),
        grid=(points // tile,),
        out_shape=(block, block),
        in_specs=[
            fixed(masks.shape),
            pl.BlockSpec((1, 2, tile, points), lambda step: (0, 0, step, 0)),
            fixed(first.shape),
            fixed(second.shape),
        ],
        out_specs=(fixed(block.shape), fixed(block.shape)),
        scratch_shapes=[pltpu.VMEM((2 * points, width), jnp.bfloat16)] * 2
        + [pltpu.VMEM((points, width), jnp.bfloat16)] * 2,
        cost_estimate=pl.CostEstimate(
            flops=24 * points * points * width, bytes_accessed=6 * points * points, transcendentals=0
        ),
        compiler_params=pltpu.CompilerParams(vmem_limit_bytes=PAIR_GRANT),
        name=f"pair_{turn_number}",
    )(masks, kernel, first, second)


def total_kernel(mesh_counts, plan_ref, *refs):
    out_ref = refs[-1]
    own = linear_of(own_places(), mesh_counts)
    out_ref[...] = jnp.zeros_like(out_ref)
    for number, block_ref in enumerate(refs[:-1]):
        cell = cell_of(plan_ref[number // 2, number % 2, own], out_ref.shape[:3])
        held = out_ref[cell[0], cell[1], cell[2]]
        out_ref[cell[0], cell[1], cell[2]] = held + block_ref[...].astype(out_ref.dtype)


def totalled(mesh_counts, cell_counts, plan, blocks):
    return pl.pallas_call(
        functools.partial(total_kernel, mesh_counts),
        out_shape=jax.ShapeDtypeStruct((*cell_counts, *blocks[0].shape), jnp.float32),
        in_specs=[whole(pltpu.SMEM)] + [whole(pltpu.VMEM)] * len(blocks),
        out_specs=whole(pltpu.VMEM),
        compiler_params=pltpu.CompilerParams(vmem_limit_bytes=SMALL_GRANT),
        name="totals",
    )(plan, *blocks)


def on_device(orbitals, kernel, plan, occupation):
    mesh_counts = mesh_sizes()
    cell_counts = orbitals.shape[:3]
    arrived = []
    for turn_number in range(plan.shape[0]):
        forward, partner = hop_shifts(turn_number, mesh_counts)
        first_send, second_send = picked(turn_number, mesh_counts, plan, orbitals)
        second = moved(second_send, partner, mesh_counts)
        first = moved(first_send, forward, mesh_counts)
        arrived.append((first, second))
    masks = masks_of(mesh_counts, cell_counts, plan, occupation)
    returned = []
    for turn_number, (first, second) in enumerate(arrived):
        forward, partner = hop_shifts(turn_number, mesh_counts)
        first_block, second_block = pair_blocks(turn_number, masks, kernel, first, second)
        returned.append(moved(first_block, negated(forward), mesh_counts))
        returned.append(moved(second_block, negated(partner), mesh_counts))
    return totalled(mesh_counts, cell_counts, plan, returned)


def solution(mesh):
    placed = (P("kx", "ky", "kz", None, None), P(("kx", "ky", "kz"), None, None, None), P(), P())
    return jax.shard_map(
        on_device,
        mesh=mesh,
        in_specs=placed,
        out_specs=P("kx", "ky", "kz", None, None),
        check_vma=False,
    )
```

```python
import functools

import jax
import jax.numpy as jnp
from jax import lax
from jax.experimental import pallas as pl
from jax.experimental.pallas import tpu as pltpu
from jax.sharding import PartitionSpec as P


AXES = ("kx", "ky", "kz")
SMALL_GRANT = 4 << 20
PICK_GRANT = 52 << 20
PAIR_GRANT = 24 << 20
CONTRACT_LAST = (((1,), (1,)), ((), ()))
CONTRACT_FIRST = (((0,), (0,)), ((), ()))


def mesh_sizes():
    return tuple(lax.axis_size(axis) for axis in AXES)


def hop_shifts(turn_number, mesh_counts):
    forward = (
        (turn_number + 1) % mesh_counts[0],
        (2 * turn_number + 1) % mesh_counts[1],
        (3 * turn_number + 1) % mesh_counts[2],
    )
    partner = (forward[0], forward[1], (forward[2] - mesh_counts[2] // 2) % mesh_counts[2])
    return (forward, partner)


def linear_of(places, mesh_counts):
    return (places[0] * mesh_counts[1] + places[1]) * mesh_counts[2] + places[2]


def moved(block, shift, mesh_counts):
    route = []
    for first in range(mesh_counts[0]):
        for second in range(mesh_counts[1]):
            for third in range(mesh_counts[2]):
                target = tuple(
                    (place + step) % count
                    for place, step, count in zip((first, second, third), shift, mesh_counts)
                )
                route.append(
                    (linear_of((first, second, third), mesh_counts), linear_of(target, mesh_counts))
                )
    return lax.ppermute(block, AXES, route)


def after(block, *earlier):
    return lax.optimization_barrier((block, *earlier))[0] if earlier else block


def negated(shift):
    return tuple(-step for step in shift)


def cell_of(slot, cell_counts):
    return (
        slot // (cell_counts[1] * cell_counts[2]),
        slot // cell_counts[2] % cell_counts[1],
        slot % cell_counts[2],
    )


def own_places():
    return tuple(lax.axis_index(axis) for axis in AXES)


def wrapped(value, count):
    return jnp.where(value < 0, value + count, value)


def whole(space):
    return pl.BlockSpec(memory_space=space)


def pick_kernel(turn_number, mesh_counts, bounds, plan_ref, orbitals_ref, *refs):
    sems = refs[-1]
    own = linear_of(own_places(), mesh_counts)
    copies = []
    for number, out_ref in enumerate(refs[:-1]):
        column = 1 if number == 0 else 0
        cell = cell_of(plan_ref[turn_number, column, own], orbitals_ref.shape[:3])
        low = 0 if number == 0 else bounds[number - 1]
        copy = pltpu.make_async_copy(
            orbitals_ref.at[cell[0], cell[1], cell[2], pl.ds(low, out_ref.shape[0])],
            out_ref,
            sems.at[number],
        )
        copy.start()
        copies.append(copy)
    for copy in copies:
        copy.wait()


def picked(turn_number, mesh_counts, bounds, plan, orbitals):
    points, width = orbitals.shape[3:]
    lengths = [points] + [high - low for low, high in zip(bounds, bounds[1:])]
    return pl.pallas_call(
        functools.partial(pick_kernel, turn_number, mesh_counts, bounds),
        out_shape=tuple(jax.ShapeDtypeStruct((rows, width), orbitals.dtype) for rows in lengths),
        in_specs=[whole(pltpu.SMEM), whole(pl.ANY)],
        out_specs=(whole(pltpu.VMEM),) * len(lengths),
        scratch_shapes=[pltpu.SemaphoreType.DMA((len(lengths),))],
        compiler_params=pltpu.CompilerParams(vmem_limit_bytes=PICK_GRANT),
    )(plan, orbitals)


def mask_kernel(mesh_counts, cell_counts, plan_ref, occupation_ref, out_ref, rows, sem):
    places = own_places()
    copies = []
    turns = plan_ref.shape[0]
    for turn_number in range(turns):
        for column, shift in enumerate(hop_shifts(turn_number, mesh_counts)):
            sender = tuple(
                wrapped(place - step, count)
                for place, step, count in zip(places, shift, mesh_counts)
            )
            cell = cell_of(plan_ref[turn_number, column, linear_of(sender, mesh_counts)], cell_counts)
            point = tuple(
                place * count + inner for place, count, inner in zip(sender, cell_counts, cell)
            )
            entry = 2 * turn_number + column
            copy = pltpu.make_async_copy(
                occupation_ref.at[point[0], point[1], pl.ds(point[2], 1)],
                rows.at[pl.ds(entry, 1)],
                sem.at[entry],
            )
            copy.start()
            copies.append(copy)
    for copy in copies:
        copy.wait()
    held = rows[...].astype(jnp.float32)
    out_ref[...] = jnp.concatenate([held, held], axis=1)


def masks_of(mesh_counts, cell_counts, plan, occupation):
    entries = plan.shape[0] * 2
    bands = occupation.shape[3]
    return pl.pallas_call(
        functools.partial(mask_kernel, mesh_counts, cell_counts),
        out_shape=jax.ShapeDtypeStruct((entries, 2 * bands), jnp.float32),
        in_specs=[whole(pltpu.SMEM), whole(pl.ANY)],
        out_specs=whole(pltpu.VMEM),
        scratch_shapes=[
            pltpu.VMEM((entries, bands), occupation.dtype),
            pltpu.SemaphoreType.DMA((entries,)),
        ],
        compiler_params=pltpu.CompilerParams(vmem_limit_bytes=SMALL_GRANT),
        name="masks",
    )(plan, occupation)


def quarter_turn(block):
    bands = block.shape[1] // 2
    return jnp.concatenate([-block[:, bands:], block[:, :bands]], axis=1)


def folded(gram):
    bands = gram.shape[0] // 2
    top, bottom = gram[:bands], gram[bands:]
    return -(top + jnp.concatenate([bottom[:, bands:], -bottom[:, :bands]], axis=1))


def dot32(left, right, dims):
    return lax.dot_general(left, right, dims, preferred_element_type=jnp.float32)


def unturned(block):
    bands = block.shape[1] // 2
    return jnp.concatenate([block[:, bands:], -block[:, :bands]], axis=1)


def both_parts(rows_of, mask):
    masked = rows_of * mask
    return jnp.concatenate([masked, unturned(masked)], axis=0)


def steps(low, high, size):
    return [(start, min(start + size, high)) for start in range(low, high, size)]


def weigh_kernel(turn_number, mask_ref, kernel_ref, second_ref, weighed_ref, wide_ref):
    points = second_ref.shape[0]
    size = points // 4
    wide_ref[:points] = second_ref[...]
    wide_ref[points:] = quarter_turn(second_ref[...])
    entry = 2 * turn_number + 1
    mask = mask_ref[entry : entry + 1, :].astype(second_ref.dtype)
    for low, high in steps(0, points, size):
        left = both_parts(second_ref[low:high], mask)
        for start, stop in steps(0, points, size):
            density = dot32(left, second_ref[start:stop], CONTRACT_LAST)
            real, imag = density[: high - low], density[high - low :]
            weight_real = kernel_ref[0, 0, low:high, start:stop].astype(jnp.float32)
            weight_imag = kernel_ref[0, 1, low:high, start:stop].astype(jnp.float32)
            weighed_ref[low:high, start:stop] = (weight_real * real - weight_imag * imag).astype(
                jnp.bfloat16
            )
            weighed_ref[low:high, points + start : points + stop] = (
                weight_real * imag + weight_imag * real
            ).astype(jnp.bfloat16)


def pair_call(body, out_shape, scratch, flops, operands, aliases=None):
    return pl.pallas_call(
        body,
        out_shape=out_shape,
        in_specs=[whole(pltpu.VMEM)] * len(operands),
        out_specs=jax.tree.map(lambda _: whole(pltpu.VMEM), out_shape),
        scratch_shapes=scratch,
        input_output_aliases=aliases or {},
        cost_estimate=pl.CostEstimate(flops=flops, bytes_accessed=0, transcendentals=0),
        compiler_params=pltpu.CompilerParams(vmem_limit_bytes=PAIR_GRANT),
    )(*operands)


def weighed_by(turn_number, masks, kernel, second):
    points, width = second.shape
    return pair_call(
        functools.partial(weigh_kernel, turn_number),
        (
            jax.ShapeDtypeStruct((points, 2 * points), jnp.bfloat16),
            jax.ShapeDtypeStruct((2 * points, width), second.dtype),
        ),
        [],
        4 * points * points * width,
        (masks, kernel, second),
    )


def first_kernel(bounds, stage, *refs):
    low, high = bounds[stage : stage + 2]
    last = stage == len(bounds) - 2
    weighed_ref, refs = refs[0], refs[1:]
    pieces, refs = refs[: stage + 1] if last else refs[:1], refs[stage + 1 :] if last else refs[1:]
    earlier_ref = refs[0] if stage else None
    out_ref, mixed_ref = (refs[-2], refs[-1]) if last else (refs[-1], refs[-1])
    points = weighed_ref.shape[0]
    piece = pieces[-1][...]
    right = jnp.concatenate([piece, quarter_turn(piece)], axis=0)
    plain = (((1,), (0,)), ((), ()))
    for start, stop in steps(0, points, points // 4):
        left = jnp.concatenate(
            [weighed_ref[start:stop, low:high], weighed_ref[start:stop, points + low : points + high]],
            axis=1,
        )
        part = dot32(left, right, plain)
        if stage:
            part = part + earlier_ref[start:stop]
        mixed_ref[start:stop] = part.astype(mixed_ref.dtype)
    if last:
        gram = None
        for number, block_ref in enumerate(pieces):
            rows = slice(bounds[number], bounds[number + 1])
            part = dot32(block_ref[...], mixed_ref[rows], CONTRACT_FIRST)
            gram = part if gram is None else gram + part
        out_ref[...] = folded(gram).astype(out_ref.dtype)


def first_mixed(bounds, stage, weighed, pieces, earlier):
    points = weighed.shape[0]
    width = pieces[0].shape[1]
    last = stage == len(bounds) - 2
    operands = (weighed, *(pieces if last else pieces[-1:]))
    aliases = {}
    if stage:
        operands += (earlier,)
        aliases = {} if last else {len(operands) - 1: 0}
    shape = (width // 2, width) if last else (points, width)
    out = jax.ShapeDtypeStruct(shape, jnp.bfloat16 if last else jnp.float32)
    return pair_call(
        functools.partial(first_kernel, bounds, stage),
        out,
        [pltpu.VMEM((points, width), jnp.bfloat16)] if last else [],
        8 * points * (bounds[stage + 1] - bounds[stage]) * width,
        operands,
        aliases,
    )


def second_kernel(turn_number, bounds, stage, mask_ref, kernel_ref, wide_ref, *refs):
    pieces, refs = refs[: stage + 1], refs[stage + 1 :]
    last = stage == len(bounds) - 2
    _, high = bounds[stage : stage + 2]
    earlier_ref = refs[0] if stage else None
    held_ref, out_ref = refs[-1], refs[-3] if last else refs[-2]
    mixed_ref = refs[-2] if last else out_ref
    points = wide_ref.shape[0] // 2
    size = points // 4
    plain = (((1,), (0,)), ((), ()))
    entry = 2 * turn_number
    mask = mask_ref[entry : entry + 1, :].astype(wide_ref.dtype)
    slot = 0
    for number, rows_ref in enumerate(pieces):
        column_pieces = range(stage + 1) if number == stage else range(stage, stage + 1)
        column_low = bounds[column_pieces[0]]
        span = high - column_low
        for start, stop in steps(0, rows_ref.shape[0], size):
            row_low, row_high = bounds[number] + start, bounds[number] + stop
            count = stop - start
            left = both_parts(rows_ref[start:stop], mask)
            for column in column_pieces:
                for begin, end in steps(0, pieces[column].shape[0], size):
                    density = dot32(left, pieces[column][begin:end], CONTRACT_LAST)
                    real, imag = density[:count], density[count:]
                    columns = slice(bounds[column] + begin, bounds[column] + end)
                    at = bounds[column] + begin - column_low
                    weight_real = kernel_ref[0, 0, row_low:row_high, columns].astype(jnp.float32)
                    weight_imag = kernel_ref[0, 1, row_low:row_high, columns].astype(jnp.float32)
                    held_ref[slot, :count, at : at + end - begin] = (
                        weight_real * real + weight_imag * imag
                    ).astype(jnp.bfloat16)
                    held_ref[slot, :count, span + at : span + at + end - begin] = (
                        weight_real * imag - weight_imag * real
                    ).astype(jnp.bfloat16)
            if column_low:
                right = jnp.concatenate(
                    [wide_ref[column_low:high], wide_ref[points + column_low : points + high]], axis=0
                )
                part = dot32(held_ref[slot, :count, : 2 * span], right, plain)
            elif high == points:
                part = dot32(held_ref[slot, :count], wide_ref[...], plain)
            else:
                right = jnp.concatenate([wide_ref[:high], wide_ref[points : points + high]], axis=0)
                part = dot32(held_ref[slot, :count, : 2 * span], right, plain)
            if number < stage:
                part = part + earlier_ref[row_low:row_high]
            mixed_ref[row_low:row_high] = part.astype(mixed_ref.dtype)
            slot = 1 - slot
    if last:
        out_ref[...] = folded(dot32(wide_ref[:points], mixed_ref[...], CONTRACT_FIRST)).astype(
            out_ref.dtype
        )


def second_mixed(turn_number, bounds, stage, masks, kernel, wide, pieces, earlier):
    points, width = wide.shape[0] // 2, wide.shape[1]
    last = stage == len(bounds) - 2
    high, low = bounds[stage + 1], bounds[stage]
    operands = (masks, kernel, wide, *pieces)
    aliases = {}
    if stage:
        operands += (earlier,)
    shape = (width // 2, width) if last else (high, width)
    out = jax.ShapeDtypeStruct(shape, jnp.bfloat16 if last else jnp.float32)
    scratch = [pltpu.VMEM((2, points // 4, 2 * high), jnp.bfloat16)]
    if last:
        scratch = [pltpu.VMEM((points, width), jnp.bfloat16)] + scratch
    return pair_call(
        functools.partial(second_kernel, turn_number, bounds, stage),
        out,
        scratch,
        12 * (high * high - low * low) * width,
        operands,
        aliases,
    )


def total_kernel(mesh_counts, plan_ref, *refs):
    out_ref = refs[-1]
    own = linear_of(own_places(), mesh_counts)
    out_ref[...] = jnp.zeros_like(out_ref)
    for number, pair_ref in enumerate(refs[:-1]):
        turn_number = plan_ref.shape[0] - 1 - number
        for column in range(2):
            cell = cell_of(plan_ref[turn_number, 1 - column, own], out_ref.shape[:3])
            held = out_ref[cell[0], cell[1], cell[2]]
            out_ref[cell[0], cell[1], cell[2]] = held + pair_ref[column].astype(out_ref.dtype)


def totalled(mesh_counts, cell_counts, plan, pairs):
    return pl.pallas_call(
        functools.partial(total_kernel, mesh_counts),
        out_shape=jax.ShapeDtypeStruct((*cell_counts, *pairs[0].shape[1:]), jnp.float32),
        in_specs=[whole(pltpu.SMEM)] + [whole(pltpu.VMEM)] * len(pairs),
        out_specs=whole(pltpu.VMEM),
        compiler_params=pltpu.CompilerParams(vmem_limit_bytes=SMALL_GRANT),
        name="totals",
    )(plan, *pairs)


def on_device(orbitals, kernel, plan, occupation):
    mesh_counts = mesh_sizes()
    cell_counts = orbitals.shape[:3]
    turns = plan.shape[0]
    points = orbitals.shape[3]
    half = (0, 0, mesh_counts[2] // 2)
    order = tuple(reversed(range(turns)))
    bounds_of = {turn_number: (0, points) for turn_number in order}
    bounds_of[order[-1]] = (0, points // 2, points)
    sends = {
        turn_number: picked(turn_number, mesh_counts, bounds_of[turn_number], plan, orbitals)
        for turn_number in order
    }
    masks = masks_of(mesh_counts, cell_counts, plan, occupation)
    returned = {}
    done_before = ()
    for turn_number in order:
        bounds = bounds_of[turn_number]
        forward, partner = hop_shifts(turn_number, mesh_counts)
        second = moved(sends[turn_number][0], partner, mesh_counts)
        arrived = []
        for send in sends[turn_number][1:]:
            arrived.append(moved(send, forward, mesh_counts))
        weighed, wide = weighed_by(
            turn_number, after(masks, *done_before), kernel, second
        )
        first_block = second_block = None
        for stage in range(len(bounds) - 1):
            pieces = arrived[: stage + 1]
            if stage:
                weighed = after(weighed, second_block)
            first_block = first_mixed(bounds, stage, weighed, pieces, first_block)
            if stage == len(bounds) - 2:
                crossed = moved(first_block, half, mesh_counts)
            second_block = second_mixed(
                turn_number, bounds, stage, masks, kernel, wide, pieces, second_block
            )
        done_before = (second_block,)
        returned[turn_number] = moved(
            jnp.stack([second_block, crossed]), negated(partner), mesh_counts
        )
    blocks = [returned[turn_number] for turn_number in reversed(range(turns))]
    return totalled(mesh_counts, cell_counts, plan, blocks)


def solution(mesh):
    placed = (P("kx", "ky", "kz", None, None), P(("kx", "ky", "kz"), None, None, None), P(), P())

    return jax.shard_map(
        on_device,
        mesh=mesh,
        in_specs=placed,
        out_specs=P("kx", "ky", "kz", None, None),
        check_vma=False,
    )
```

```python
import functools

import jax
import jax.numpy as jnp
from jax import lax
from jax.experimental import pallas as pl
from jax.experimental.pallas import tpu as pltpu
from jax.sharding import PartitionSpec as P


AXES = ("kx", "ky", "kz")
SMALL_GRANT = 4 << 20
PICK_GRANT = 52 << 20
PAIR_GRANT = 24 << 20
WIDEN_GRANT = 24 << 20
WEIGH_ROWS = 4
WEIGH_COLS = 4
SECOND_TALL = 4
SECOND_ROWS = 4
SECOND_COLS = 4
CONTRACT_LAST = (((1,), (1,)), ((), ()))
CONTRACT_FIRST = (((0,), (0,)), ((), ()))


def mesh_sizes():
    return tuple(lax.axis_size(axis) for axis in AXES)


def hop_shifts(turn_number, mesh_counts):
    forward = (
        (turn_number + 1) % mesh_counts[0],
        (2 * turn_number + 1) % mesh_counts[1],
        (3 * turn_number + 1) % mesh_counts[2],
    )
    partner = (forward[0], forward[1], (forward[2] - mesh_counts[2] // 2) % mesh_counts[2])
    return (forward, partner)


def linear_of(places, mesh_counts):
    return (places[0] * mesh_counts[1] + places[1]) * mesh_counts[2] + places[2]


def moved(block, shift, mesh_counts):
    route = []
    for first in range(mesh_counts[0]):
        for second in range(mesh_counts[1]):
            for third in range(mesh_counts[2]):
                target = tuple(
                    (place + step) % count
                    for place, step, count in zip((first, second, third), shift, mesh_counts)
                )
                route.append(
                    (linear_of((first, second, third), mesh_counts), linear_of(target, mesh_counts))
                )
    return lax.ppermute(block, AXES, route)


def after(block, *earlier):
    return lax.optimization_barrier((block, *earlier))[0] if earlier else block


def negated(shift):
    return tuple(-step for step in shift)


def cell_of(slot, cell_counts):
    return (
        slot // (cell_counts[1] * cell_counts[2]),
        slot // cell_counts[2] % cell_counts[1],
        slot % cell_counts[2],
    )


def own_places():
    return tuple(lax.axis_index(axis) for axis in AXES)


def wrapped(value, count):
    return jnp.where(value < 0, value + count, value)


def whole(space):
    return pl.BlockSpec(memory_space=space)


def pick_kernel(turn_number, mesh_counts, bounds, plan_ref, orbitals_ref, *refs):
    sems = refs[-1]
    own = linear_of(own_places(), mesh_counts)
    copies = []
    for number, out_ref in enumerate(refs[:-1]):
        column = 1 if number == 0 else 0
        cell = cell_of(plan_ref[turn_number, column, own], orbitals_ref.shape[:3])
        low = 0 if number == 0 else bounds[number - 1]
        copy = pltpu.make_async_copy(
            orbitals_ref.at[cell[0], cell[1], cell[2], pl.ds(low, out_ref.shape[0])],
            out_ref,
            sems.at[number],
        )
        copy.start()
        copies.append(copy)
    for copy in copies:
        copy.wait()


def picked(turn_number, mesh_counts, bounds, plan, orbitals):
    points, width = orbitals.shape[3:]
    lengths = [points] + [high - low for low, high in zip(bounds, bounds[1:])]
    return pl.pallas_call(
        functools.partial(pick_kernel, turn_number, mesh_counts, bounds),
        out_shape=tuple(jax.ShapeDtypeStruct((rows, width), orbitals.dtype) for rows in lengths),
        in_specs=[whole(pltpu.SMEM), whole(pl.ANY)],
        out_specs=(whole(pltpu.VMEM),) * len(lengths),
        scratch_shapes=[pltpu.SemaphoreType.DMA((len(lengths),))],
        compiler_params=pltpu.CompilerParams(vmem_limit_bytes=PICK_GRANT),
    )(plan, orbitals)


def mask_kernel(mesh_counts, cell_counts, plan_ref, occupation_ref, out_ref, rows, sem):
    places = own_places()
    copies = []
    turns = plan_ref.shape[0]
    for turn_number in range(turns):
        for column, shift in enumerate(hop_shifts(turn_number, mesh_counts)):
            sender = tuple(
                wrapped(place - step, count)
                for place, step, count in zip(places, shift, mesh_counts)
            )
            cell = cell_of(plan_ref[turn_number, column, linear_of(sender, mesh_counts)], cell_counts)
            point = tuple(
                place * count + inner for place, count, inner in zip(sender, cell_counts, cell)
            )
            entry = 2 * turn_number + column
            copy = pltpu.make_async_copy(
                occupation_ref.at[point[0], point[1], pl.ds(point[2], 1)],
                rows.at[pl.ds(entry, 1)],
                sem.at[entry],
            )
            copy.start()
            copies.append(copy)
    for copy in copies:
        copy.wait()
    held = rows[...].astype(jnp.float32)
    out_ref[...] = jnp.concatenate([held, held], axis=1)


def masks_of(mesh_counts, cell_counts, plan, occupation):
    entries = plan.shape[0] * 2
    bands = occupation.shape[3]
    return pl.pallas_call(
        functools.partial(mask_kernel, mesh_counts, cell_counts),
        out_shape=jax.ShapeDtypeStruct((entries, 2 * bands), jnp.float32),
        in_specs=[whole(pltpu.SMEM), whole(pl.ANY)],
        out_specs=whole(pltpu.VMEM),
        scratch_shapes=[
            pltpu.VMEM((entries, bands), occupation.dtype),
            pltpu.SemaphoreType.DMA((entries,)),
        ],
        compiler_params=pltpu.CompilerParams(vmem_limit_bytes=SMALL_GRANT),
        name="masks",
    )(plan, occupation)


def quarter_turn(block):
    bands = block.shape[1] // 2
    wide = pltpu.roll(block.astype(jnp.float32), bands, 1)
    lane = lax.broadcasted_iota(jnp.int32, (1, block.shape[1]), 1)
    return (wide * jnp.where(lane < bands, -1.0, 1.0)).astype(block.dtype)


def folded(gram):
    bands = gram.shape[0] // 2
    top, bottom = gram[:bands], gram[bands:]
    return -(top + jnp.concatenate([bottom[:, bands:], -bottom[:, :bands]], axis=1))


def dot32(left, right, dims):
    return lax.dot_general(left, right, dims, preferred_element_type=jnp.float32)


def steps(low, high, size):
    return [(start, min(start + size, high)) for start in range(low, high, size)]


def weigh_kernel(turn_number, mask_ref, kernel_ref, second_ref, weighed_ref, wide_ref):
    points = second_ref.shape[0]
    wide_ref[:points] = second_ref[...]
    wide_ref[points:] = quarter_turn(second_ref[...])
    entry = 2 * turn_number + 1
    mask = mask_ref[entry : entry + 1, :].astype(second_ref.dtype)
    for start, stop in steps(0, points, points // WEIGH_COLS):
        right = second_ref[start:stop]
        for low, high in steps(0, points, points // WEIGH_ROWS):
            real = dot32(second_ref[low:high] * mask, right, CONTRACT_LAST)
            imag = dot32(wide_ref[points + low : points + high] * -mask, right, CONTRACT_LAST)
            weight_real = kernel_ref[0, low:high, start:stop]
            weight_imag = kernel_ref[1, low:high, start:stop]
            weighed_ref[low:high, start:stop] = (weight_real * real - weight_imag * imag).astype(
                jnp.bfloat16
            )
            weighed_ref[low:high, points + start : points + stop] = (
                weight_real * imag + weight_imag * real
            ).astype(jnp.bfloat16)


def widen_kernel(kernel_ref, out_ref):
    out_ref[...] = kernel_ref[0].astype(jnp.float32)


def widened(kernel):
    parts, rows, columns = kernel.shape[1:]
    size = rows // 4
    return pl.pallas_call(
        widen_kernel,
        grid=(rows // size,),
        out_shape=jax.ShapeDtypeStruct((parts, rows, columns), jnp.float32),
        in_specs=[pl.BlockSpec((1, parts, size, columns), lambda step: (0, 0, step, 0))],
        out_specs=pl.BlockSpec((parts, size, columns), lambda step: (0, step, 0)),
        compiler_params=pltpu.CompilerParams(vmem_limit_bytes=WIDEN_GRANT),
        name="widen",
    )(kernel)


def pair_call(body, out_shape, scratch, flops, operands, aliases=None):
    return pl.pallas_call(
        body,
        out_shape=out_shape,
        in_specs=[whole(pltpu.VMEM)] * len(operands),
        out_specs=jax.tree.map(lambda _: whole(pltpu.VMEM), out_shape),
        scratch_shapes=scratch,
        input_output_aliases=aliases or {},
        cost_estimate=pl.CostEstimate(flops=flops, bytes_accessed=0, transcendentals=0),
        compiler_params=pltpu.CompilerParams(vmem_limit_bytes=PAIR_GRANT),
    )(*operands)


def weighed_by(turn_number, masks, kernel, second):
    points, width = second.shape
    return pair_call(
        functools.partial(weigh_kernel, turn_number),
        (
            jax.ShapeDtypeStruct((points, 2 * points), jnp.bfloat16),
            jax.ShapeDtypeStruct((2 * points, width), second.dtype),
        ),
        [],
        4 * points * points * width,
        (masks, kernel, second),
    )


def first_kernel(bounds, stage, *refs):
    low, high = bounds[stage : stage + 2]
    last = stage == len(bounds) - 2
    weighed_ref, refs = refs[0], refs[1:]
    pieces, refs = refs[: stage + 1] if last else refs[:1], refs[stage + 1 :] if last else refs[1:]
    earlier_ref = refs[0] if stage else None
    out_ref, mixed_ref = (refs[-2], refs[-1]) if last else (refs[-1], refs[-1])
    points = weighed_ref.shape[0]
    piece = pieces[-1][...]
    right = jnp.concatenate([piece, quarter_turn(piece)], axis=0)
    plain = (((1,), (0,)), ((), ()))
    for start, stop in steps(0, points, points // 4):
        left = jnp.concatenate(
            [weighed_ref[start:stop, low:high], weighed_ref[start:stop, points + low : points + high]],
            axis=1,
        )
        part = dot32(left, right, plain)
        if stage:
            part = part + earlier_ref[start:stop]
        mixed_ref[start:stop] = part.astype(mixed_ref.dtype)
    if last:
        gram = None
        for number, block_ref in enumerate(pieces):
            rows = slice(bounds[number], bounds[number + 1])
            part = dot32(block_ref[...], mixed_ref[rows], CONTRACT_FIRST)
            gram = part if gram is None else gram + part
        out_ref[...] = folded(gram).astype(out_ref.dtype)


def first_mixed(bounds, stage, weighed, pieces, earlier):
    points = weighed.shape[0]
    width = pieces[0].shape[1]
    last = stage == len(bounds) - 2
    operands = (weighed, *(pieces if last else pieces[-1:]))
    aliases = {}
    if stage:
        operands += (earlier,)
        aliases = {} if last else {len(operands) - 1: 0}
    shape = (width // 2, width) if last else (points, width)
    out = jax.ShapeDtypeStruct(shape, jnp.bfloat16 if last else jnp.float32)
    return pair_call(
        functools.partial(first_kernel, bounds, stage),
        out,
        [pltpu.VMEM((points, width), jnp.bfloat16)] if last else [],
        8 * points * (bounds[stage + 1] - bounds[stage]) * width,
        operands,
        aliases,
    )


def second_kernel(turn_number, bounds, stage, mask_ref, kernel_ref, wide_ref, *refs):
    pieces, refs = refs[: stage + 1], refs[stage + 1 :]
    last = stage == len(bounds) - 2
    _, high = bounds[stage : stage + 2]
    earlier_ref = refs[0] if stage else None
    held_ref, out_ref = refs[-1], refs[-3] if last else refs[-2]
    mixed_ref = refs[-2] if last else out_ref
    points = wide_ref.shape[0] // 2
    plain = (((1,), (0,)), ((), ()))
    entry = 2 * turn_number
    mask = mask_ref[entry : entry + 1, :].astype(wide_ref.dtype)
    slot = 0
    for number, rows_ref in enumerate(pieces):
        column_pieces = range(stage + 1) if number == stage else range(stage, stage + 1)
        column_low = bounds[column_pieces[0]]
        span = high - column_low
        if column_low or high < points:
            right = jnp.concatenate(
                [wide_ref[column_low:high], wide_ref[points + column_low : points + high]], axis=0
            )
        else:
            right = wide_ref[...]
        for start, stop in steps(0, rows_ref.shape[0], points // SECOND_TALL):
            turned = quarter_turn(rows_ref[start:stop]) * -mask
            kept = rows_ref[start:stop] * mask
            for column in column_pieces:
                for begin, end in steps(0, pieces[column].shape[0], points // SECOND_COLS):
                    across = pieces[column][begin:end]
                    columns = slice(bounds[column] + begin, bounds[column] + end)
                    at = bounds[column] + begin - column_low
                    for top, bottom in steps(0, stop - start, points // SECOND_ROWS):
                        real = dot32(kept[top:bottom], across, CONTRACT_LAST)
                        imag = dot32(turned[top:bottom], across, CONTRACT_LAST)
                        rows = slice(
                            bounds[number] + start + top, bounds[number] + start + bottom
                        )
                        weight_real = kernel_ref[0, rows, columns]
                        weight_imag = kernel_ref[1, rows, columns]
                        held_ref[slot, top:bottom, at : at + end - begin] = (
                            weight_real * real + weight_imag * imag
                        ).astype(jnp.bfloat16)
                        held_ref[slot, top:bottom, span + at : span + at + end - begin] = (
                            weight_real * imag - weight_imag * real
                        ).astype(jnp.bfloat16)
            part = dot32(held_ref[slot, : stop - start, : 2 * span], right, plain)
            rows = slice(bounds[number] + start, bounds[number] + stop)
            if number < stage:
                part = part + earlier_ref[rows]
            mixed_ref[rows] = part.astype(mixed_ref.dtype)
            slot = 1 - slot
    if last:
        out_ref[...] = folded(dot32(wide_ref[:points], mixed_ref[...], CONTRACT_FIRST)).astype(
            out_ref.dtype
        )


def second_mixed(turn_number, bounds, stage, masks, kernel, wide, pieces, earlier):
    points, width = wide.shape[0] // 2, wide.shape[1]
    last = stage == len(bounds) - 2
    high, low = bounds[stage + 1], bounds[stage]
    operands = (masks, kernel, wide, *pieces)
    aliases = {}
    if stage:
        operands += (earlier,)
    shape = (width // 2, width) if last else (high, width)
    out = jax.ShapeDtypeStruct(shape, jnp.bfloat16 if last else jnp.float32)
    scratch = [pltpu.VMEM((2, points // SECOND_TALL, 2 * high), jnp.bfloat16)]
    if last:
        scratch = [pltpu.VMEM((points, width), jnp.bfloat16)] + scratch
    return pair_call(
        functools.partial(second_kernel, turn_number, bounds, stage),
        out,
        scratch,
        12 * (high * high - low * low) * width,
        operands,
        aliases,
    )


def total_kernel(mesh_counts, plan_ref, *refs):
    out_ref = refs[-1]
    own = linear_of(own_places(), mesh_counts)
    out_ref[...] = jnp.zeros_like(out_ref)
    for number, pair_ref in enumerate(refs[:-1]):
        turn_number = plan_ref.shape[0] - 1 - number
        for column in range(2):
            cell = cell_of(plan_ref[turn_number, 1 - column, own], out_ref.shape[:3])
            held = out_ref[cell[0], cell[1], cell[2]]
            out_ref[cell[0], cell[1], cell[2]] = held + pair_ref[column].astype(out_ref.dtype)


def totalled(mesh_counts, cell_counts, plan, pairs):
    return pl.pallas_call(
        functools.partial(total_kernel, mesh_counts),
        out_shape=jax.ShapeDtypeStruct((*cell_counts, *pairs[0].shape[1:]), jnp.float32),
        in_specs=[whole(pltpu.SMEM)] + [whole(pltpu.VMEM)] * len(pairs),
        out_specs=whole(pltpu.VMEM),
        compiler_params=pltpu.CompilerParams(vmem_limit_bytes=SMALL_GRANT),
        name="totals",
    )(plan, *pairs)


def on_device(orbitals, kernel, plan, occupation):
    mesh_counts = mesh_sizes()
    cell_counts = orbitals.shape[:3]
    turns = plan.shape[0]
    points = orbitals.shape[3]
    half = (0, 0, mesh_counts[2] // 2)
    order = tuple(reversed(range(turns)))
    bounds_of = {turn_number: (0, points) for turn_number in order}
    bounds_of[order[-1]] = (0, points // 2, points * 3 // 4, points)
    sends = {
        turn_number: picked(turn_number, mesh_counts, bounds_of[turn_number], plan, orbitals)
        for turn_number in order
    }
    masks = masks_of(mesh_counts, cell_counts, plan, occupation)
    kernel = widened(after(kernel, masks))
    returned = {}
    done_before = ()
    for turn_number in order:
        bounds = bounds_of[turn_number]
        forward, partner = hop_shifts(turn_number, mesh_counts)
        second = moved(sends[turn_number][0], partner, mesh_counts)
        arrived = []
        for send in sends[turn_number][1:]:
            arrived.append(moved(send, forward, mesh_counts))
        weighed, wide = weighed_by(
            turn_number, after(masks, *done_before), kernel, second
        )
        first_block = second_block = None
        for stage in range(len(bounds) - 1):
            pieces = arrived[: stage + 1]
            if stage:
                weighed = after(weighed, second_block)
            first_block = first_mixed(bounds, stage, weighed, pieces, first_block)
            if stage == len(bounds) - 2:
                crossed = moved(first_block, half, mesh_counts)
            second_block = second_mixed(
                turn_number, bounds, stage, masks, kernel, wide, pieces, second_block
            )
        done_before = (second_block,)
        returned[turn_number] = moved(
            jnp.stack([second_block, crossed]), negated(partner), mesh_counts
        )
    blocks = [returned[turn_number] for turn_number in reversed(range(turns))]
    return totalled(mesh_counts, cell_counts, plan, blocks)


def solution(mesh):
    placed = (P("kx", "ky", "kz", None, None), P(("kx", "ky", "kz"), None, None, None), P(), P())

    return jax.shard_map(
        on_device,
        mesh=mesh,
        in_specs=placed,
        out_specs=P("kx", "ky", "kz", None, None),
        check_vma=False,
    )
```

```python
import functools

import jax
import jax.numpy as jnp
from jax import lax
from jax.experimental import pallas as pl
from jax.experimental.pallas import tpu as pltpu
from jax.sharding import PartitionSpec as P


AXES = ("kx", "ky", "kz")
SMALL_GRANT = 4 << 20
PICK_GRANT = 52 << 20
PAIR_GRANT = 24 << 20
WIDEN_GRANT = 24 << 20
WEIGH_ROWS = 4
WEIGH_COLS = 4
SECOND_TALL = 4
SECOND_ROWS = 4
SECOND_COLS = 4
CONTRACT_LAST = (((1,), (1,)), ((), ()))
CONTRACT_FIRST = (((0,), (0,)), ((), ()))


def mesh_sizes():
    return tuple(lax.axis_size(axis) for axis in AXES)


def hop_shifts(turn_number, mesh_counts):
    forward = (
        (turn_number + 1) % mesh_counts[0],
        (2 * turn_number + 1) % mesh_counts[1],
        (3 * turn_number + 1) % mesh_counts[2],
    )
    partner = (forward[0], forward[1], (forward[2] - mesh_counts[2] // 2) % mesh_counts[2])
    return (forward, partner)


def linear_of(places, mesh_counts):
    return (places[0] * mesh_counts[1] + places[1]) * mesh_counts[2] + places[2]


def moved(block, shift, mesh_counts):
    route = []
    for first in range(mesh_counts[0]):
        for second in range(mesh_counts[1]):
            for third in range(mesh_counts[2]):
                target = tuple(
                    (place + step) % count
                    for place, step, count in zip((first, second, third), shift, mesh_counts)
                )
                route.append(
                    (linear_of((first, second, third), mesh_counts), linear_of(target, mesh_counts))
                )
    return lax.ppermute(block, AXES, route)


def after(block, *earlier):
    return lax.optimization_barrier((block, *earlier))[0] if earlier else block


def negated(shift):
    return tuple(-step for step in shift)


def cell_of(slot, cell_counts):
    return (
        slot // (cell_counts[1] * cell_counts[2]),
        slot // cell_counts[2] % cell_counts[1],
        slot % cell_counts[2],
    )


def own_places():
    return tuple(lax.axis_index(axis) for axis in AXES)


def wrapped(value, count):
    return jnp.where(value < 0, value + count, value)


def slot_of(plan_ref, turn_number, column, device):
    row = plan_ref[turn_number, column : column + 1, :]
    lane = lax.broadcasted_iota(jnp.int32, row.shape, 1)
    return jnp.sum(jnp.where(lane == device, row, 0))


def whole(space):
    return pl.BlockSpec(memory_space=space)


def pick_kernel(turn_number, mesh_counts, bounds, plan_ref, orbitals_ref, *refs):
    sems = refs[-1]
    own = linear_of(own_places(), mesh_counts)
    slots = [slot_of(plan_ref, turn_number, column, own) for column in range(2)]
    copies = []
    for number, out_ref in enumerate(refs[:-1]):
        column = 1 if number == 0 else 0
        cell = cell_of(slots[column], orbitals_ref.shape[:3])
        low = 0 if number == 0 else bounds[number - 1]
        copy = pltpu.make_async_copy(
            orbitals_ref.at[cell[0], cell[1], cell[2], pl.ds(low, out_ref.shape[0])],
            out_ref,
            sems.at[number],
        )
        copy.start()
        copies.append(copy)
    for copy in copies:
        copy.wait()


def picked(turn_number, mesh_counts, bounds, plan, orbitals):
    points, width = orbitals.shape[3:]
    lengths = [points] + [high - low for low, high in zip(bounds, bounds[1:])]
    return pl.pallas_call(
        functools.partial(pick_kernel, turn_number, mesh_counts, bounds),
        out_shape=tuple(jax.ShapeDtypeStruct((rows, width), orbitals.dtype) for rows in lengths),
        in_specs=[whole(pltpu.VMEM), whole(pl.ANY)],
        out_specs=(whole(pltpu.VMEM),) * len(lengths),
        scratch_shapes=[pltpu.SemaphoreType.DMA((len(lengths),))],
        compiler_params=pltpu.CompilerParams(vmem_limit_bytes=PICK_GRANT),
    )(plan, orbitals)


def mask_kernel(mesh_counts, cell_counts, plan_ref, occupation_ref, out_ref, rows, sem):
    places = own_places()
    copies = []
    turns = plan_ref.shape[0]
    for turn_number in range(turns):
        for column, shift in enumerate(hop_shifts(turn_number, mesh_counts)):
            sender = tuple(
                wrapped(place - step, count)
                for place, step, count in zip(places, shift, mesh_counts)
            )
            cell = cell_of(plan_ref[turn_number, column, linear_of(sender, mesh_counts)], cell_counts)
            point = tuple(
                place * count + inner for place, count, inner in zip(sender, cell_counts, cell)
            )
            entry = 2 * turn_number + column
            copy = pltpu.make_async_copy(
                occupation_ref.at[point[0], point[1], pl.ds(point[2], 1)],
                rows.at[pl.ds(entry, 1)],
                sem.at[entry],
            )
            copy.start()
            copies.append(copy)
    for copy in copies:
        copy.wait()
    held = rows[...].astype(jnp.float32)
    out_ref[...] = jnp.concatenate([held, held], axis=1)


def masks_of(mesh_counts, cell_counts, plan, occupation):
    entries = plan.shape[0] * 2
    bands = occupation.shape[3]
    return pl.pallas_call(
        functools.partial(mask_kernel, mesh_counts, cell_counts),
        out_shape=jax.ShapeDtypeStruct((entries, 2 * bands), jnp.float32),
        in_specs=[whole(pltpu.SMEM), whole(pl.ANY)],
        out_specs=whole(pltpu.VMEM),
        scratch_shapes=[
            pltpu.VMEM((entries, bands), occupation.dtype),
            pltpu.SemaphoreType.DMA((entries,)),
        ],
        compiler_params=pltpu.CompilerParams(vmem_limit_bytes=SMALL_GRANT),
        name="masks",
    )(plan, occupation)


def quarter_turn(block):
    bands = block.shape[1] // 2
    wide = pltpu.roll(block.astype(jnp.float32), bands, 1)
    lane = lax.broadcasted_iota(jnp.int32, (1, block.shape[1]), 1)
    return (wide * jnp.where(lane < bands, -1.0, 1.0)).astype(block.dtype)


def folded(gram):
    bands = gram.shape[0] // 2
    top, bottom = gram[:bands], gram[bands:]
    return -(top + jnp.concatenate([bottom[:, bands:], -bottom[:, :bands]], axis=1))


def dot32(left, right, dims):
    return lax.dot_general(left, right, dims, preferred_element_type=jnp.float32)


def steps(low, high, size):
    return [(start, min(start + size, high)) for start in range(low, high, size)]


def weigh_kernel(turn_number, mask_ref, kernel_ref, second_ref, weighed_ref, wide_ref):
    points = second_ref.shape[0]
    wide_ref[:points] = second_ref[...]
    wide_ref[points:] = quarter_turn(second_ref[...])
    entry = 2 * turn_number + 1
    mask = mask_ref[entry : entry + 1, :].astype(second_ref.dtype)
    for start, stop in steps(0, points, points // WEIGH_COLS):
        right = second_ref[start:stop]
        for low, high in steps(0, points, points // WEIGH_ROWS):
            real = dot32(second_ref[low:high] * mask, right, CONTRACT_LAST)
            imag = dot32(wide_ref[points + low : points + high] * -mask, right, CONTRACT_LAST)
            weight_real = kernel_ref[0, low:high, start:stop]
            weight_imag = kernel_ref[1, low:high, start:stop]
            weighed_ref[low:high, start:stop] = (weight_real * real - weight_imag * imag).astype(
                jnp.bfloat16
            )
            weighed_ref[low:high, points + start : points + stop] = (
                weight_real * imag + weight_imag * real
            ).astype(jnp.bfloat16)


def widen_kernel(kernel_ref, out_ref):
    out_ref[...] = kernel_ref[0].astype(jnp.float32)


def widened(kernel):
    parts, rows, columns = kernel.shape[1:]
    size = rows // 4
    return pl.pallas_call(
        widen_kernel,
        grid=(rows // size,),
        out_shape=jax.ShapeDtypeStruct((parts, rows, columns), jnp.float32),
        in_specs=[pl.BlockSpec((1, parts, size, columns), lambda step: (0, 0, step, 0))],
        out_specs=pl.BlockSpec((parts, size, columns), lambda step: (0, step, 0)),
        compiler_params=pltpu.CompilerParams(vmem_limit_bytes=WIDEN_GRANT),
        name="widen",
    )(kernel)


def pair_call(body, out_shape, scratch, flops, operands, aliases=None):
    return pl.pallas_call(
        body,
        out_shape=out_shape,
        in_specs=[whole(pltpu.VMEM)] * len(operands),
        out_specs=jax.tree.map(lambda _: whole(pltpu.VMEM), out_shape),
        scratch_shapes=scratch,
        input_output_aliases=aliases or {},
        cost_estimate=pl.CostEstimate(flops=flops, bytes_accessed=0, transcendentals=0),
        compiler_params=pltpu.CompilerParams(vmem_limit_bytes=PAIR_GRANT),
    )(*operands)


def weighed_by(turn_number, masks, kernel, second):
    points, width = second.shape
    return pair_call(
        functools.partial(weigh_kernel, turn_number),
        (
            jax.ShapeDtypeStruct((points, 2 * points), jnp.bfloat16),
            jax.ShapeDtypeStruct((2 * points, width), second.dtype),
        ),
        [],
        4 * points * points * width,
        (masks, kernel, second),
    )


def first_kernel(bounds, stage, *refs):
    low, high = bounds[stage : stage + 2]
    last = stage == len(bounds) - 2
    weighed_ref, refs = refs[0], refs[1:]
    pieces, refs = refs[: stage + 1] if last else refs[:1], refs[stage + 1 :] if last else refs[1:]
    earlier_ref = refs[0] if stage else None
    out_ref, mixed_ref = (refs[-2], refs[-1]) if last else (refs[-1], refs[-1])
    points = weighed_ref.shape[0]
    piece = pieces[-1][...]
    right = jnp.concatenate([piece, quarter_turn(piece)], axis=0)
    plain = (((1,), (0,)), ((), ()))
    for start, stop in steps(0, points, points // 4):
        left = jnp.concatenate(
            [weighed_ref[start:stop, low:high], weighed_ref[start:stop, points + low : points + high]],
            axis=1,
        )
        part = dot32(left, right, plain)
        if stage:
            part = part + earlier_ref[start:stop]
        mixed_ref[start:stop] = part.astype(mixed_ref.dtype)
    if last:
        gram = None
        for number, block_ref in enumerate(pieces):
            rows = slice(bounds[number], bounds[number + 1])
            part = dot32(block_ref[...], mixed_ref[rows], CONTRACT_FIRST)
            gram = part if gram is None else gram + part
        out_ref[...] = folded(gram).astype(out_ref.dtype)


def first_mixed(bounds, stage, weighed, pieces, earlier):
    points = weighed.shape[0]
    width = pieces[0].shape[1]
    last = stage == len(bounds) - 2
    operands = (weighed, *(pieces if last else pieces[-1:]))
    aliases = {}
    if stage:
        operands += (earlier,)
        aliases = {} if last else {len(operands) - 1: 0}
    shape = (width // 2, width) if last else (points, width)
    out = jax.ShapeDtypeStruct(shape, jnp.bfloat16 if last else jnp.float32)
    return pair_call(
        functools.partial(first_kernel, bounds, stage),
        out,
        [pltpu.VMEM((points, width), jnp.bfloat16)] if last else [],
        8 * points * (bounds[stage + 1] - bounds[stage]) * width,
        operands,
        aliases,
    )


def second_kernel(turn_number, bounds, stage, mask_ref, kernel_ref, wide_ref, *refs):
    pieces, refs = refs[: stage + 1], refs[stage + 1 :]
    last = stage == len(bounds) - 2
    _, high = bounds[stage : stage + 2]
    earlier_ref = refs[0] if stage else None
    held_ref, out_ref = refs[-1], refs[-3] if last else refs[-2]
    mixed_ref = refs[-2] if last else out_ref
    points = wide_ref.shape[0] // 2
    plain = (((1,), (0,)), ((), ()))
    entry = 2 * turn_number
    mask = mask_ref[entry : entry + 1, :].astype(wide_ref.dtype)
    slot = 0
    for number, rows_ref in enumerate(pieces):
        column_pieces = range(stage + 1) if number == stage else range(stage, stage + 1)
        column_low = bounds[column_pieces[0]]
        span = high - column_low
        if column_low or high < points:
            right = jnp.concatenate(
                [wide_ref[column_low:high], wide_ref[points + column_low : points + high]], axis=0
            )
        else:
            right = wide_ref[...]
        for start, stop in steps(0, rows_ref.shape[0], points // SECOND_TALL):
            turned = quarter_turn(rows_ref[start:stop]) * -mask
            kept = rows_ref[start:stop] * mask
            for column in column_pieces:
                for begin, end in steps(0, pieces[column].shape[0], points // SECOND_COLS):
                    across = pieces[column][begin:end]
                    columns = slice(bounds[column] + begin, bounds[column] + end)
                    at = bounds[column] + begin - column_low
                    for top, bottom in steps(0, stop - start, points // SECOND_ROWS):
                        real = dot32(kept[top:bottom], across, CONTRACT_LAST)
                        imag = dot32(turned[top:bottom], across, CONTRACT_LAST)
                        rows = slice(
                            bounds[number] + start + top, bounds[number] + start + bottom
                        )
                        weight_real = kernel_ref[0, rows, columns]
                        weight_imag = kernel_ref[1, rows, columns]
                        held_ref[slot, top:bottom, at : at + end - begin] = (
                            weight_real * real + weight_imag * imag
                        ).astype(jnp.bfloat16)
                        held_ref[slot, top:bottom, span + at : span + at + end - begin] = (
                            weight_real * imag - weight_imag * real
                        ).astype(jnp.bfloat16)
            part = dot32(held_ref[slot, : stop - start, : 2 * span], right, plain)
            rows = slice(bounds[number] + start, bounds[number] + stop)
            if number < stage:
                part = part + earlier_ref[rows]
            mixed_ref[rows] = part.astype(mixed_ref.dtype)
            slot = 1 - slot
    if last:
        out_ref[...] = folded(dot32(wide_ref[:points], mixed_ref[...], CONTRACT_FIRST)).astype(
            out_ref.dtype
        )


def second_mixed(turn_number, bounds, stage, masks, kernel, wide, pieces, earlier):
    points, width = wide.shape[0] // 2, wide.shape[1]
    last = stage == len(bounds) - 2
    high, low = bounds[stage + 1], bounds[stage]
    operands = (masks, kernel, wide, *pieces)
    aliases = {}
    if stage:
        operands += (earlier,)
    shape = (width // 2, width) if last else (high, width)
    out = jax.ShapeDtypeStruct(shape, jnp.bfloat16 if last else jnp.float32)
    scratch = [pltpu.VMEM((2, points // SECOND_TALL, 2 * high), jnp.bfloat16)]
    if last:
        scratch = [pltpu.VMEM((points, width), jnp.bfloat16)] + scratch
    return pair_call(
        functools.partial(second_kernel, turn_number, bounds, stage),
        out,
        scratch,
        12 * (high * high - low * low) * width,
        operands,
        aliases,
    )


def total_kernel(mesh_counts, plan_ref, *refs):
    out_ref = refs[-1]
    own = linear_of(own_places(), mesh_counts)
    out_ref[...] = jnp.zeros_like(out_ref)
    for number, pair_ref in enumerate(refs[:-1]):
        turn_number = plan_ref.shape[0] - 1 - number
        for column in range(2):
            cell = cell_of(slot_of(plan_ref, turn_number, 1 - column, own), out_ref.shape[:3])
            held = out_ref[cell[0], cell[1], cell[2]]
            out_ref[cell[0], cell[1], cell[2]] = held + pair_ref[column].astype(out_ref.dtype)


def totalled(mesh_counts, cell_counts, plan, pairs):
    return pl.pallas_call(
        functools.partial(total_kernel, mesh_counts),
        out_shape=jax.ShapeDtypeStruct((*cell_counts, *pairs[0].shape[1:]), jnp.float32),
        in_specs=[whole(pltpu.VMEM)] * (1 + len(pairs)),
        out_specs=whole(pltpu.VMEM),
        compiler_params=pltpu.CompilerParams(vmem_limit_bytes=SMALL_GRANT),
        name="totals",
    )(plan, *pairs)


def on_device(orbitals, kernel, plan, occupation):
    mesh_counts = mesh_sizes()
    cell_counts = orbitals.shape[:3]
    turns = plan.shape[0]
    points = orbitals.shape[3]
    half = (0, 0, mesh_counts[2] // 2)
    order = tuple(reversed(range(turns)))
    bounds_of = {turn_number: (0, points) for turn_number in order}
    bounds_of[order[-1]] = (0, points // 2, points * 3 // 4, points)
    sends = {
        turn_number: picked(turn_number, mesh_counts, bounds_of[turn_number], plan, orbitals)
        for turn_number in order
    }
    masks = masks_of(mesh_counts, cell_counts, plan, occupation)
    kernel = widened(after(kernel, masks))
    returned = {}
    done_before = ()
    for turn_number in order:
        bounds = bounds_of[turn_number]
        forward, partner = hop_shifts(turn_number, mesh_counts)
        second = moved(sends[turn_number][0], partner, mesh_counts)
        arrived = []
        for send in sends[turn_number][1:]:
            arrived.append(moved(send, forward, mesh_counts))
        weighed, wide = weighed_by(
            turn_number, after(masks, *done_before), kernel, second
        )
        first_block = second_block = None
        for stage in range(len(bounds) - 1):
            pieces = arrived[: stage + 1]
            if stage:
                weighed = after(weighed, second_block)
            first_block = first_mixed(bounds, stage, weighed, pieces, first_block)
            if stage == len(bounds) - 2:
                crossed = moved(first_block, half, mesh_counts)
            second_block = second_mixed(
                turn_number, bounds, stage, masks, kernel, wide, pieces, second_block
            )
        done_before = (second_block,)
        returned[turn_number] = moved(
            jnp.stack([second_block, crossed]), negated(partner), mesh_counts
        )
    blocks = [returned[turn_number] for turn_number in reversed(range(turns))]
    return totalled(mesh_counts, cell_counts, plan, blocks)


def solution(mesh):
    placed = (P("kx", "ky", "kz", None, None), P(("kx", "ky", "kz"), None, None, None), P(), P())

    return jax.shard_map(
        on_device,
        mesh=mesh,
        in_specs=placed,
        out_specs=P("kx", "ky", "kz", None, None),
        check_vma=False,
    )
```

```python
import functools

import jax
import jax.numpy as jnp
from jax import lax
from jax.experimental import pallas as pl
from jax.experimental.pallas import tpu as pltpu
from jax.sharding import PartitionSpec as P


AXES = ("kx", "ky", "kz")
SMALL_GRANT = 4 << 20
PICK_GRANT = 52 << 20
PAIR_GRANT = 24 << 20
WIDEN_GRANT = 24 << 20
WEIGH_ROWS = 4
WEIGH_COLS = 4
SECOND_TALL = 4
SECOND_ROWS = 4
SECOND_COLS = 4
CONTRACT_LAST = (((1,), (1,)), ((), ()))
CONTRACT_FIRST = (((0,), (0,)), ((), ()))


def mesh_sizes():
    return tuple(lax.axis_size(axis) for axis in AXES)


def hop_shifts(turn_number, mesh_counts):
    forward = (
        (turn_number + 1) % mesh_counts[0],
        (2 * turn_number + 1) % mesh_counts[1],
        (3 * turn_number + 1) % mesh_counts[2],
    )
    partner = (forward[0], forward[1], (forward[2] - mesh_counts[2] // 2) % mesh_counts[2])
    return (forward, partner)


def linear_of(places, mesh_counts):
    return (places[0] * mesh_counts[1] + places[1]) * mesh_counts[2] + places[2]


def moved(block, shift, mesh_counts):
    route = []
    for first in range(mesh_counts[0]):
        for second in range(mesh_counts[1]):
            for third in range(mesh_counts[2]):
                target = tuple(
                    (place + step) % count
                    for place, step, count in zip((first, second, third), shift, mesh_counts)
                )
                route.append(
                    (linear_of((first, second, third), mesh_counts), linear_of(target, mesh_counts))
                )
    return lax.ppermute(block, AXES, route)


def after(block, *earlier):
    return lax.optimization_barrier((block, *earlier))[0] if earlier else block


def negated(shift):
    return tuple(-step for step in shift)


def cell_of(slot, cell_counts):
    return (
        slot // (cell_counts[1] * cell_counts[2]),
        slot // cell_counts[2] % cell_counts[1],
        slot % cell_counts[2],
    )


def own_places():
    return tuple(lax.axis_index(axis) for axis in AXES)


def wrapped(value, count):
    return jnp.where(value < 0, value + count, value)


def slot_of(plan_ref, turn_number, column, device):
    row = plan_ref[turn_number, column : column + 1, :]
    lane = lax.broadcasted_iota(jnp.int32, row.shape, 1)
    return jnp.sum(jnp.where(lane == device, row, 0))


def whole(space):
    return pl.BlockSpec(memory_space=space)


def pick_kernel(jobs, mesh_counts, plan_ref, orbitals_ref, *refs):
    sems = refs[-1]
    own = linear_of(own_places(), mesh_counts)
    slots = {}
    copies = []
    for number, (turn_number, column, low) in enumerate(jobs):
        if (turn_number, column) not in slots:
            slots[turn_number, column] = slot_of(plan_ref, turn_number, column, own)
        cell = cell_of(slots[turn_number, column], orbitals_ref.shape[:3])
        copy = pltpu.make_async_copy(
            orbitals_ref.at[cell[0], cell[1], cell[2], pl.ds(low, refs[number].shape[0])],
            refs[number],
            sems.at[number],
        )
        copy.start()
        copies.append(copy)
    for copy in copies:
        copy.wait()


def picked(bounds_of, mesh_counts, plan, orbitals):
    points, width = orbitals.shape[3:]
    jobs, lengths = [], []
    for turn_number, bounds in bounds_of.items():
        jobs.append((turn_number, 1, 0))
        lengths.append(points)
        jobs += [(turn_number, 0, low) for low in bounds[:-1]]
        lengths += [high - low for low, high in zip(bounds, bounds[1:])]
    blocks = pl.pallas_call(
        functools.partial(pick_kernel, tuple(jobs), mesh_counts),
        out_shape=tuple(jax.ShapeDtypeStruct((rows, width), orbitals.dtype) for rows in lengths),
        in_specs=[whole(pltpu.VMEM), whole(pl.ANY)],
        out_specs=(whole(pltpu.VMEM),) * len(lengths),
        scratch_shapes=[pltpu.SemaphoreType.DMA((len(lengths),))],
        compiler_params=pltpu.CompilerParams(vmem_limit_bytes=PICK_GRANT),
        name="pick",
    )(plan, orbitals)
    sends = {turn_number: [] for turn_number in bounds_of}
    for job, block in zip(jobs, blocks):
        sends[job[0]].append(block)
    return sends


def mask_kernel(mesh_counts, cell_counts, plan_ref, occupation_ref, out_ref, rows, sem):
    places = own_places()
    copies = []
    turns = plan_ref.shape[0]
    for turn_number in range(turns):
        for column, shift in enumerate(hop_shifts(turn_number, mesh_counts)):
            sender = tuple(
                wrapped(place - step, count)
                for place, step, count in zip(places, shift, mesh_counts)
            )
            cell = cell_of(plan_ref[turn_number, column, linear_of(sender, mesh_counts)], cell_counts)
            point = tuple(
                place * count + inner for place, count, inner in zip(sender, cell_counts, cell)
            )
            entry = 2 * turn_number + column
            copy = pltpu.make_async_copy(
                occupation_ref.at[point[0], point[1], pl.ds(point[2], 1)],
                rows.at[pl.ds(entry, 1)],
                sem.at[entry],
            )
            copy.start()
            copies.append(copy)
    for copy in copies:
        copy.wait()
    held = rows[...].astype(jnp.float32)
    out_ref[...] = jnp.concatenate([held, held], axis=1)


def masks_of(mesh_counts, cell_counts, plan, occupation):
    entries = plan.shape[0] * 2
    bands = occupation.shape[3]
    return pl.pallas_call(
        functools.partial(mask_kernel, mesh_counts, cell_counts),
        out_shape=jax.ShapeDtypeStruct((entries, 2 * bands), jnp.float32),
        in_specs=[whole(pltpu.SMEM), whole(pl.ANY)],
        out_specs=whole(pltpu.VMEM),
        scratch_shapes=[
            pltpu.VMEM((entries, bands), occupation.dtype),
            pltpu.SemaphoreType.DMA((entries,)),
        ],
        compiler_params=pltpu.CompilerParams(vmem_limit_bytes=SMALL_GRANT),
        name="masks",
    )(plan, occupation)


def quarter_turn(block):
    bands = block.shape[1] // 2
    wide = pltpu.roll(block.astype(jnp.float32), bands, 1)
    lane = lax.broadcasted_iota(jnp.int32, (1, block.shape[1]), 1)
    return (wide * jnp.where(lane < bands, -1.0, 1.0)).astype(block.dtype)


def folded(gram):
    bands = gram.shape[0] // 2
    top, bottom = gram[:bands], gram[bands:]
    return -(top + jnp.concatenate([bottom[:, bands:], -bottom[:, :bands]], axis=1))


def dot32(left, right, dims):
    return lax.dot_general(left, right, dims, preferred_element_type=jnp.float32)


def steps(low, high, size):
    return [(start, min(start + size, high)) for start in range(low, high, size)]


def weigh_kernel(turn_number, mask_ref, kernel_ref, second_ref, weighed_ref, wide_ref):
    points = second_ref.shape[0]
    wide_ref[:points] = second_ref[...]
    wide_ref[points:] = quarter_turn(second_ref[...])
    entry = 2 * turn_number + 1
    mask = mask_ref[entry : entry + 1, :].astype(second_ref.dtype)
    for start, stop in steps(0, points, points // WEIGH_COLS):
        right = second_ref[start:stop]
        for low, high in steps(0, points, points // WEIGH_ROWS):
            real = dot32(second_ref[low:high] * mask, right, CONTRACT_LAST)
            imag = dot32(wide_ref[points + low : points + high] * -mask, right, CONTRACT_LAST)
            weight_real = kernel_ref[0, low:high, start:stop]
            weight_imag = kernel_ref[1, low:high, start:stop]
            weighed_ref[low:high, start:stop] = (weight_real * real - weight_imag * imag).astype(
                jnp.bfloat16
            )
            weighed_ref[low:high, points + start : points + stop] = (
                weight_real * imag + weight_imag * real
            ).astype(jnp.bfloat16)


def widen_kernel(kernel_ref, out_ref):
    out_ref[...] = kernel_ref[0].astype(jnp.float32)


def widened(kernel):
    parts, rows, columns = kernel.shape[1:]
    size = rows // 4
    return pl.pallas_call(
        widen_kernel,
        grid=(rows // size,),
        out_shape=jax.ShapeDtypeStruct((parts, rows, columns), jnp.float32),
        in_specs=[pl.BlockSpec((1, parts, size, columns), lambda step: (0, 0, step, 0))],
        out_specs=pl.BlockSpec((parts, size, columns), lambda step: (0, step, 0)),
        compiler_params=pltpu.CompilerParams(vmem_limit_bytes=WIDEN_GRANT),
        name="widen",
    )(kernel)


def pair_call(body, out_shape, scratch, flops, operands, aliases=None):
    return pl.pallas_call(
        body,
        out_shape=out_shape,
        in_specs=[whole(pltpu.VMEM)] * len(operands),
        out_specs=jax.tree.map(lambda _: whole(pltpu.VMEM), out_shape),
        scratch_shapes=scratch,
        input_output_aliases=aliases or {},
        cost_estimate=pl.CostEstimate(flops=flops, bytes_accessed=0, transcendentals=0),
        compiler_params=pltpu.CompilerParams(vmem_limit_bytes=PAIR_GRANT),
    )(*operands)


def weighed_by(turn_number, masks, kernel, second):
    points, width = second.shape
    return pair_call(
        functools.partial(weigh_kernel, turn_number),
        (
            jax.ShapeDtypeStruct((points, 2 * points), jnp.bfloat16),
            jax.ShapeDtypeStruct((2 * points, width), second.dtype),
        ),
        [],
        4 * points * points * width,
        (masks, kernel, second),
    )


def first_kernel(bounds, stage, *refs):
    low, high = bounds[stage : stage + 2]
    last = stage == len(bounds) - 2
    weighed_ref, refs = refs[0], refs[1:]
    pieces, refs = refs[: stage + 1] if last else refs[:1], refs[stage + 1 :] if last else refs[1:]
    earlier_ref = refs[0] if stage else None
    out_ref, mixed_ref = (refs[-2], refs[-1]) if last else (refs[-1], refs[-1])
    points = weighed_ref.shape[0]
    piece = pieces[-1][...]
    right = jnp.concatenate([piece, quarter_turn(piece)], axis=0)
    plain = (((1,), (0,)), ((), ()))
    for start, stop in steps(0, points, points // 4):
        left = jnp.concatenate(
            [weighed_ref[start:stop, low:high], weighed_ref[start:stop, points + low : points + high]],
            axis=1,
        )
        part = dot32(left, right, plain)
        if stage:
            part = part + earlier_ref[start:stop]
        mixed_ref[start:stop] = part.astype(mixed_ref.dtype)
    if last:
        gram = None
        for number, block_ref in enumerate(pieces):
            rows = slice(bounds[number], bounds[number + 1])
            part = dot32(block_ref[...], mixed_ref[rows], CONTRACT_FIRST)
            gram = part if gram is None else gram + part
        out_ref[...] = folded(gram).astype(out_ref.dtype)


def first_mixed(bounds, stage, weighed, pieces, earlier):
    points = weighed.shape[0]
    width = pieces[0].shape[1]
    last = stage == len(bounds) - 2
    operands = (weighed, *(pieces if last else pieces[-1:]))
    aliases = {}
    if stage:
        operands += (earlier,)
        aliases = {} if last else {len(operands) - 1: 0}
    shape = (width // 2, width) if last else (points, width)
    out = jax.ShapeDtypeStruct(shape, jnp.bfloat16 if last else jnp.float32)
    return pair_call(
        functools.partial(first_kernel, bounds, stage),
        out,
        [pltpu.VMEM((points, width), jnp.bfloat16)] if last else [],
        8 * points * (bounds[stage + 1] - bounds[stage]) * width,
        operands,
        aliases,
    )


def second_kernel(turn_number, bounds, stage, mask_ref, kernel_ref, wide_ref, *refs):
    pieces, refs = refs[: stage + 1], refs[stage + 1 :]
    last = stage == len(bounds) - 2
    _, high = bounds[stage : stage + 2]
    earlier_ref = refs[0] if stage else None
    held_ref, out_ref = refs[-1], refs[-3] if last else refs[-2]
    mixed_ref = refs[-2] if last else out_ref
    points = wide_ref.shape[0] // 2
    plain = (((1,), (0,)), ((), ()))
    entry = 2 * turn_number
    mask = mask_ref[entry : entry + 1, :].astype(wide_ref.dtype)
    slot = 0
    for number, rows_ref in enumerate(pieces):
        column_pieces = range(stage + 1) if number == stage else range(stage, stage + 1)
        column_low = bounds[column_pieces[0]]
        span = high - column_low
        if column_low or high < points:
            right = jnp.concatenate(
                [wide_ref[column_low:high], wide_ref[points + column_low : points + high]], axis=0
            )
        else:
            right = wide_ref[...]
        for start, stop in steps(0, rows_ref.shape[0], points // SECOND_TALL):
            turned = quarter_turn(rows_ref[start:stop]) * -mask
            kept = rows_ref[start:stop] * mask
            for column in column_pieces:
                for begin, end in steps(0, pieces[column].shape[0], points // SECOND_COLS):
                    across = pieces[column][begin:end]
                    columns = slice(bounds[column] + begin, bounds[column] + end)
                    at = bounds[column] + begin - column_low
                    for top, bottom in steps(0, stop - start, points // SECOND_ROWS):
                        real = dot32(kept[top:bottom], across, CONTRACT_LAST)
                        imag = dot32(turned[top:bottom], across, CONTRACT_LAST)
                        rows = slice(
                            bounds[number] + start + top, bounds[number] + start + bottom
                        )
                        weight_real = kernel_ref[0, rows, columns]
                        weight_imag = kernel_ref[1, rows, columns]
                        held_ref[slot, top:bottom, at : at + end - begin] = (
                            weight_real * real + weight_imag * imag
                        ).astype(jnp.bfloat16)
                        held_ref[slot, top:bottom, span + at : span + at + end - begin] = (
                            weight_real * imag - weight_imag * real
                        ).astype(jnp.bfloat16)
            part = dot32(held_ref[slot, : stop - start, : 2 * span], right, plain)
            rows = slice(bounds[number] + start, bounds[number] + stop)
            if number < stage:
                part = part + earlier_ref[rows]
            mixed_ref[rows] = part.astype(mixed_ref.dtype)
            slot = 1 - slot
    if last:
        out_ref[...] = folded(dot32(wide_ref[:points], mixed_ref[...], CONTRACT_FIRST)).astype(
            out_ref.dtype
        )


def second_mixed(turn_number, bounds, stage, masks, kernel, wide, pieces, earlier):
    points, width = wide.shape[0] // 2, wide.shape[1]
    last = stage == len(bounds) - 2
    high, low = bounds[stage + 1], bounds[stage]
    operands = (masks, kernel, wide, *pieces)
    aliases = {}
    if stage:
        operands += (earlier,)
    shape = (width // 2, width) if last else (high, width)
    out = jax.ShapeDtypeStruct(shape, jnp.bfloat16 if last else jnp.float32)
    scratch = [pltpu.VMEM((2, points // SECOND_TALL, 2 * high), jnp.bfloat16)]
    if last:
        scratch = [pltpu.VMEM((points, width), jnp.bfloat16)] + scratch
    return pair_call(
        functools.partial(second_kernel, turn_number, bounds, stage),
        out,
        scratch,
        12 * (high * high - low * low) * width,
        operands,
        aliases,
    )


def base_kernel(mesh_counts, plan_ref, *refs):
    pairs, (out_ref, held_ref) = refs[:-2], refs[-2:]
    own = linear_of(own_places(), mesh_counts)
    out_ref[...] = jnp.zeros_like(out_ref)
    for number, pair_ref in enumerate(pairs):
        turn_number = number + 1
        for column in range(2):
            cell = cell_of(slot_of(plan_ref, turn_number, 1 - column, own), out_ref.shape[:3])
            held = out_ref[cell[0], cell[1], cell[2]]
            out_ref[cell[0], cell[1], cell[2]] = held + pair_ref[column].astype(out_ref.dtype)
    for column in range(2):
        cell = cell_of(slot_of(plan_ref, 0, 1 - column, own), out_ref.shape[:3])
        held_ref[column] = out_ref[cell[0], cell[1], cell[2]]


def based(mesh_counts, cell_counts, plan, pairs):
    block = pairs[0].shape[1:]
    return pl.pallas_call(
        functools.partial(base_kernel, mesh_counts),
        out_shape=(
            jax.ShapeDtypeStruct((*cell_counts, *block), jnp.float32),
            jax.ShapeDtypeStruct((2, *block), jnp.float32),
        ),
        in_specs=[whole(pltpu.VMEM)] * (1 + len(pairs)),
        out_specs=(whole(pltpu.VMEM), whole(pltpu.VMEM)),
        compiler_params=pltpu.CompilerParams(vmem_limit_bytes=SMALL_GRANT),
        name="base",
    )(plan, *pairs)


def total_kernel(mesh_counts, plan_ref, held_ref, pair_ref, base_ref, out_ref, sums, sems):
    own = linear_of(own_places(), mesh_counts)
    slots = [slot_of(plan_ref, 0, 1 - column, own) for column in range(2)]
    apart = slots[0] != slots[1]
    share = jnp.where(apart, 0.0, 1.0)
    blocks = [pair_ref[column].astype(out_ref.dtype) for column in range(2)]
    copies = []
    for column in range(2):
        sums[column] = held_ref[column] + (blocks[column] + share * blocks[1 - column])
        cell = cell_of(slots[column], out_ref.shape[:3])
        copies.append(
            pltpu.make_async_copy(
                sums.at[column], out_ref.at[cell[0], cell[1], cell[2]], sems.at[column]
            )
        )
    copies[0].start()
    pl.when(apart)(copies[1].start)
    copies[0].wait()
    pl.when(apart)(copies[1].wait)


def totalled(mesh_counts, plan, held, pair, base):
    return pl.pallas_call(
        functools.partial(total_kernel, mesh_counts),
        out_shape=jax.ShapeDtypeStruct(base.shape, base.dtype),
        in_specs=[whole(pltpu.VMEM)] * 3 + [whole(pl.ANY)],
        out_specs=whole(pl.ANY),
        scratch_shapes=[pltpu.VMEM(held.shape, held.dtype), pltpu.SemaphoreType.DMA((2,))],
        input_output_aliases={3: 0},
        compiler_params=pltpu.CompilerParams(vmem_limit_bytes=SMALL_GRANT),
        name="totals",
    )(plan, held, pair, base)


def on_device(orbitals, kernel, plan, occupation):
    mesh_counts = mesh_sizes()
    cell_counts = orbitals.shape[:3]
    turns = plan.shape[0]
    points = orbitals.shape[3]
    half = (0, 0, mesh_counts[2] // 2)
    order = tuple(reversed(range(turns)))
    bounds_of = {turn_number: (0, points) for turn_number in order}
    bounds_of[order[-1]] = (0, points // 2, points * 3 // 4, points)
    sends = picked(bounds_of, mesh_counts, plan, orbitals)
    masks = masks_of(mesh_counts, cell_counts, plan, occupation)
    kernel = widened(after(kernel, masks))
    returned = {}
    done_before = ()
    for turn_number in order:
        bounds = bounds_of[turn_number]
        forward, partner = hop_shifts(turn_number, mesh_counts)
        second = moved(sends[turn_number][0], partner, mesh_counts)
        arrived = []
        for send in sends[turn_number][1:]:
            arrived.append(moved(send, forward, mesh_counts))
        weighed, wide = weighed_by(
            turn_number, after(masks, *done_before), kernel, second
        )
        first_block = second_block = None
        for stage in range(len(bounds) - 1):
            pieces = arrived[: stage + 1]
            if stage:
                weighed = after(weighed, second_block)
            first_block = first_mixed(bounds, stage, weighed, pieces, first_block)
            if stage == len(bounds) - 2:
                crossed = moved(first_block, half, mesh_counts)
            second_block = second_mixed(
                turn_number, bounds, stage, masks, kernel, wide, pieces, second_block
            )
        done_before = (second_block,)
        returned[turn_number] = moved(
            jnp.stack([second_block, crossed]), negated(partner), mesh_counts
        )
    base, held = based(
        mesh_counts, cell_counts, plan, [returned[turn_number] for turn_number in range(1, turns)]
    )
    return totalled(mesh_counts, plan, held, returned[0], base)


def solution(mesh):
    placed = (P("kx", "ky", "kz", None, None), P(("kx", "ky", "kz"), None, None, None), P(), P())

    return jax.shard_map(
        on_device,
        mesh=mesh,
        in_specs=placed,
        out_specs=P("kx", "ky", "kz", None, None),
        check_vma=False,
    )
```
